32 devices in a mesh: grid: 8 (over y, x, core), pt: 4 (over z).
Axes of the slice: x: 2, y: 2, z: 4, core: 2. Of those that a mesh axis runs over, the one named last changes fastest.
Arguments:
- orbitals: bfloat16 [2048, 4096], P('grid'), may hold values from -0.875 to 0.875
- point_index: int32 [2048], P('pt'), may hold values from 0 to 4095, as said below
- factor_panels: float32 [2048, 1024], P('pt'), as said below
Outputs:
- solved: float32 [4096, 2048], P('grid', 'pt')
The draws below stay inside these ranges and needn't reach their ends.
Inputs may be any that keep to these rules, and one draw needn't show every extreme that they name: `point_index`: all entries are different; 0 and 4095 are always among them. `factor_panels`: lower triangular in its global row and column indices, diagonal between 1.5 and 3.
All inputs are finite; a program needn't handle non-finite values.
Results may differ from the reference program's by a relative error of at most 0.0018.
Values may be sent and summed in bfloat16 or wider, within the bound.
A program may use at most 64 MiB of HBM per device.

```python
import math
import jax
import jax.numpy as jnp
from jax import lax

NORB = 2048
PANEL = 512
ROWS = 4096
NPTS = 2048


def draw_point_index(key, part):
    first_key, second_key = jax.random.split(jax.random.fold_in(key, 11))
    inner = jax.random.permutation(first_key, ROWS - 2)[:NPTS - 2].astype(jnp.int32) + 1
    ends = jnp.array([0, ROWS - 1], jnp.int32)
    chosen = jnp.concatenate([ends, inner])
    return jax.random.permutation(second_key, chosen).astype(jnp.int32)


def draw_factor_panels(key, part):
    first_key, second_key = jax.random.split(jax.random.fold_in(key, 23))
    row_ids = jnp.arange(NPTS)[:, None]
    col_ids = jnp.arange(2 * PANEL)[None, :]
    sigma = 0.6 / jnp.sqrt(2.0 * PANEL)
    off_diag = jax.random.normal(first_key, (NPTS, 2 * PANEL), jnp.float32) * sigma
    diag_vals = jnp.exp(jax.random.uniform(second_key, (NPTS, 1), jnp.float32, jnp.log(1.5), jnp.log(3.0)))
    lowered = jnp.where(col_ids < row_ids, off_diag, jnp.where(col_ids == row_ids, diag_vals, 0.0))
    return lowered.astype(jnp.float32)


def level_of(rng, extent, shards, smallest, top_value):
    gain, own = 1.0, jax.random.fold_in(rng, 6)
    for axis_at, parts in shards:
        draws = jnp.exp(jax.random.uniform(jax.random.fold_in(own, axis_at), (parts,), jnp.float32, smallest / len(shards), top_value / len(shards)))
        gain = gain * jnp.repeat(draws, extent[axis_at] // parts).reshape([-1 if axis == axis_at else 1 for axis in range(len(extent))])
    return gain


def scatter_about(stream_key, extent, spread, reach, cuts=(), dtype=jnp.bfloat16):
    values = jax.random.normal(stream_key, extent, jnp.float32) * spread
    if len(cuts) > 0:
        values = level_of(stream_key, extent, cuts, -0.22, 0.18) * values
    return jnp.clip(values, min=-reach, max=reach).astype(dtype)


def setup_inputs(seed: int = 0) -> dict:
    keys = jax.random.split(jax.random.key(seed), 4)
    return {
        "orbitals": scatter_about(keys[0], (NORB, ROWS), (NORB ** -0.25), 0.875, ((0, 8),)),
        "point_index": draw_point_index(jax.random.fold_in(keys[3], 71), 0),
        "factor_panels": draw_factor_panels(jax.random.fold_in(keys[3], 71), 0),
    }


def solve_panel(factor, targets):
    return lax.linalg.triangular_solve(factor, targets, left_side=False, lower=True, transpose_a=True)

def rounded(values):
    return lax.optimization_barrier(values.astype(jnp.bfloat16)).astype(jnp.float32)

def reference(orbitals, point_index, factor_panels):
    panel_cols = PANEL
    point_orbs = jnp.take(orbitals, point_index.astype(jnp.int32), axis=1).astype(jnp.float32)
    row_step = math.gcd(ROWS, 4096)
    grouped = orbitals.reshape(NORB, ROWS // row_step, row_step).transpose(1, 0, 2)
    diag_first = factor_panels[0:panel_cols, 0:panel_cols]
    diag_second = factor_panels[panel_cols:2 * panel_cols, panel_cols:2 * panel_cols]
    below_first = factor_panels[panel_cols:, 0:panel_cols]
    below_second = factor_panels[2 * panel_cols:, panel_cols:2 * panel_cols]

    def one_block(row_block):
        inner_sums = lax.dot_general(row_block.astype(jnp.float32), point_orbs.astype(jnp.float32), (((0,), (0,)), ((), ())), precision=lax.Precision.HIGHEST, preferred_element_type=jnp.float32)
        products = inner_sums * inner_sums
        first = solve_panel(diag_first, products[:, 0:panel_cols])
        left = products[:, panel_cols:] - jnp.dot(rounded(first), below_first.T, precision=lax.Precision.HIGHEST)
        second = solve_panel(diag_second, left[:, 0:panel_cols])
        trailing = left[:, panel_cols:] - jnp.dot(rounded(second), below_second.T, precision=lax.Precision.HIGHEST)
        return jnp.concatenate([first, second, trailing], axis=1)
    solved = lax.map(one_block, grouped)
    return solved.reshape(ROWS, NPTS)
```

```python
import functools
import jax
import jax.numpy as jnp
from jax import lax
from jax.experimental import pallas as pl
from jax.experimental.pallas import tpu as pltpu
from jax.sharding import PartitionSpec as P

MESH = pl.DeviceIdType.MESH
F32, BF16 = jnp.float32, jnp.bfloat16
LANES = 128


def split(value):
    high = value.astype(BF16)
    return high, (value - high.astype(F32)).astype(BF16)


def dot(a, b):
    return jnp.dot(a, b, preferred_element_type=F32)


def exact_dot(a, b):
    return jnp.dot(a, b, preferred_element_type=F32, precision=lax.Precision.HIGHEST)


def invert_lower(low, inv):
    size = low.shape[0]
    blocks = size // LANES
    row = lax.broadcasted_iota(jnp.int32, (LANES, LANES), 0)
    col = lax.broadcasted_iota(jnp.int32, (LANES, LANES), 1)
    tiles, parts = [], []
    for i in range(blocks):
        at = slice(i * LANES, (i + 1) * LANES)
        tile = low[at, at]
        tiles.append(tile)
        parts.append(jnp.where(row == col, 1.0 / jnp.where(row == col, tile, 1.0), 0.0))
    half = 1
    level = 0
    while half < LANES:
        rb, cb = row >> level, col >> level
        mask = ((rb >> 1) == (cb >> 1)) & (rb > cb)
        mids = [exact_dot(jnp.where(mask, tiles[i], 0.0), parts[i]) for i in range(blocks)]
        parts = [parts[i] - exact_dot(parts[i], mids[i]) for i in range(blocks)]
        half *= 2
        level += 1
    inv[...] = jnp.zeros_like(inv)
    for i in range(blocks):
        at = slice(i * LANES, (i + 1) * LANES)
        inv[at, at] = parts[i]
    width = LANES
    while width < size:
        for start in range(0, size, 2 * width):
            top = slice(start, start + width)
            bottom = slice(start + width, start + 2 * width)
            mid = exact_dot(low[bottom, top], inv[top, top])
            inv[bottom, top] = -exact_dot(inv[bottom, bottom], mid)
        width *= 2


def kernel(
    grid_count, pt_count, index_ref, orb, fac, out,
    orb_v, fac_v, rows, points, gathered, low, inv, a_high, a_low, b_high, b_low, firsts, seconds,
    load_sem, own_sem, row_send, row_recv, point_send, point_recv, pass_send,
    first_send, first_recv, second_send, second_recv,
):
    me = lax.axis_index("grid")
    rank = lax.axis_index("pt")
    own_bands, grid_rows = orb.shape
    chunks = rows.shape[0]
    panel = index_ref.shape[1]
    rows_here = chunks * LANES
    partner = me + 1 - 2 * lax.rem(me, 2)
    pairs = grid_count // 2

    def own_block(g):
        return pl.ds(pl.multiple_of(g * own_bands, own_bands), own_bands)

    load_orb = pltpu.make_async_copy(orb, orb_v, load_sem.at[0])
    load_fac = pltpu.make_async_copy(fac, fac_v, load_sem.at[1])
    load_orb.start()

    barrier = pltpu.get_barrier_semaphore()

    @pl.loop(1, grid_count)
    def _(k):
        other = lax.rem(me + k, grid_count)
        pl.semaphore_signal(barrier, inc=1, device_id=(other, rank), device_id_type=MESH)

    @pl.when(rank > 0)
    def _():
        pl.semaphore_signal(barrier, inc=1, device_id=(me, rank - 1), device_id_type=MESH)

    @pl.when(rank < pt_count - 1)
    def _():
        pl.semaphore_signal(barrier, inc=1, device_id=(me, rank + 1), device_id_type=MESH)

    at_end = (rank == 0) | (rank == pt_count - 1)

    @pl.when(at_end)
    def _():
        pl.semaphore_wait(barrier, grid_count)

    @pl.when(jnp.logical_not(at_end))
    def _():
        pl.semaphore_wait(barrier, grid_count + 1)

    def row_cols(g, c):
        return pl.ds(pl.multiple_of(g * rows_here + c * LANES, LANES), LANES)

    def send_rows(c):
        @pl.loop(1, grid_count)
        def _(k):
            other = lax.rem(me + k, grid_count)
            pltpu.make_async_remote_copy(
                src_ref=orb.at[:, row_cols(other, c)],
                dst_ref=rows.at[c, own_block(me), :],
                send_sem=row_send.at[c],
                recv_sem=row_recv.at[c],
                device_id=(other, rank),
                device_id_type=MESH,
            ).start()

    send_rows(0)
    owns = []
    for c in range(chunks):
        own = pltpu.make_async_copy(orb.at[:, row_cols(me, c)], rows.at[c, own_block(me), :], own_sem.at[c])
        own.start()
        owns.append(own)
    load_fac.start()
    load_orb.wait()

    depth = min(1024, grid_rows)
    gathered[...] = jnp.zeros_like(gathered)

    @pl.loop(0, grid_rows // depth)
    def _(s):
        ids = lax.broadcasted_iota(jnp.int32, (depth, panel), 0) + s * depth
        hot = jnp.where(ids == index_ref[...], 1.0, 0.0).astype(BF16)
        gathered[...] += dot(orb_v[:, pl.ds(pl.multiple_of(s * depth, depth), depth)], hot)

    points[own_block(me), :] = gathered[...].astype(BF16)

    def point_copy(g, target, send_sem):
        return pltpu.make_async_remote_copy(
            src_ref=points.at[own_block(g), :],
            dst_ref=points.at[own_block(g), :],
            send_sem=send_sem,
            recv_sem=point_recv.at[g],
            device_id=(target, rank),
            device_id_type=MESH,
        )

    @pl.loop(1, pairs)
    def _(k):
        point_copy(me, lax.rem(me + 2 * k, grid_count), point_send.at[k]).start()

    point_copy(me, partner, pass_send.at[0]).start()
    for c in range(1, chunks):
        send_rows(c)

    load_fac.wait()

    @pl.when(rank < 2)
    def _():
        start = pl.multiple_of(rank * panel, panel)
        low[...] = fac_v[:, pl.ds(start, panel)]
        invert_lower(low, inv)

    @pl.when(rank > 0)
    def _():
        a_high[...], a_low[...] = split(fac_v[:, 0:panel].T)

    @pl.when(rank == 0)
    def _():
        a_high[...], a_low[...] = split(inv[...].T)

    @pl.when(rank > 1)
    def _():
        b_high[...], b_low[...] = split(fac_v[:, panel : 2 * panel].T)

    @pl.when(rank == 1)
    def _():
        b_high[...], b_low[...] = split(inv[...].T)

    @pl.loop(1, pairs)
    def _(k):
        source = lax.rem(me + 2 * (pairs - k), grid_count)
        point_copy(source, me, point_send.at[k]).wait_recv()
        point_copy(source, partner, pass_send.at[k]).start()

    @pl.loop(0, pairs)
    def _(k):
        source = lax.rem(partner + 2 * k, grid_count)
        point_copy(source, me, pass_send.at[k]).wait_recv()

    def chain(buf, c, send_sem, recv_sem):
        return pltpu.make_async_remote_copy(
            src_ref=buf.at[c],
            dst_ref=buf.at[c],
            send_sem=send_sem.at[c],
            recv_sem=recv_sem.at[c],
            device_id=(me, rank + 1),
            device_id_type=MESH,
        )

    def solve(value, high, low_part):
        value_high, value_low = split(value)
        return dot(value_high, high[...]) + (dot(value_high, low_part[...]) + dot(value_low, high[...]))

    def apply(value, high, low_part):
        return dot(value, high[...]) + dot(value, low_part[...])

    others = pl.ds(0, (grid_count - 1) * own_bands)

    @pl.loop(0, chunks)
    def _(c):
        pltpu.make_async_copy(rows.at[c, others, :], rows.at[c, others, :], row_recv.at[c]).wait()
        pltpu.make_async_copy(
            orb.at[:, pl.ds(0, LANES)], rows.at[c, own_block(me), :], own_sem.at[c]
        ).wait()
        sums = lax.dot_general(
            rows[c], points[...], (((0,), (0,)), ((), ())), preferred_element_type=F32
        )
        here = pl.ds(pl.multiple_of(c * LANES, LANES), LANES)
        out[here, :] = sums * sums

        @pl.when(rank == 0)
        def _():
            first = solve(out[here, :], a_high, a_low)
            out[here, :] = first
            firsts[c] = first.astype(BF16)

        @pl.when(rank > 0)
        def _():
            chain(firsts, c, first_send, first_recv).wait_recv()

        @pl.when(rank < pt_count - 1)
        def _():
            chain(firsts, c, first_send, first_recv).start()

        @pl.when(rank > 0)
        def _():
            out[here, :] -= apply(firsts[c], a_high, a_low)

        @pl.when(rank == 1)
        def _():
            second = solve(out[here, :], b_high, b_low)
            out[here, :] = second
            seconds[c] = second.astype(BF16)

        @pl.when(rank > 1)
        def _():
            chain(seconds, c, second_send, second_recv).wait_recv()

        @pl.when((rank > 0) & (rank < pt_count - 1))
        def _():
            chain(seconds, c, second_send, second_recv).start()

        @pl.when(rank > 1)
        def _():
            out[here, :] -= apply(seconds[c], b_high, b_low)

    @pl.loop(0, chunks)
    def _(c):
        pltpu.make_async_copy(rows.at[c, others, :], rows.at[c, others, :], row_send.at[c]).wait()

        @pl.when(rank < pt_count - 1)
        def _():
            chain(firsts, c, first_send, first_recv).wait_send()

        @pl.when((rank > 0) & (rank < pt_count - 1))
        def _():
            chain(seconds, c, second_send, second_recv).wait_send()

    @pl.loop(1, pairs)
    def _(k):
        point_copy(me, partner, point_send.at[k]).wait_send()

    @pl.loop(0, pairs)
    def _(k):
        point_copy(me, partner, pass_send.at[k]).wait_send()


def on_device(grid_count, pt_count, orbitals, point_index, factor_panels):
    own_bands, grid_rows = orbitals.shape
    rows_here = grid_rows // grid_count
    panel = point_index.shape[0]
    chunks = rows_here // LANES
    bands = own_bands * grid_count
    vmem = pl.BlockSpec(memory_space=pltpu.VMEM)
    hbm = pl.BlockSpec(memory_space=pl.ANY)
    dma = pltpu.SemaphoreType.DMA
    return pl.pallas_call(
        functools.partial(kernel, grid_count, pt_count),
        out_shape=jax.ShapeDtypeStruct((rows_here, panel), F32),
        in_specs=[vmem, hbm, hbm],
        out_specs=vmem,
        scratch_shapes=[
            pltpu.VMEM((own_bands, grid_rows), BF16),
            pltpu.VMEM(factor_panels.shape, F32),
            pltpu.VMEM((chunks, bands, LANES), BF16),
            pltpu.VMEM((bands, panel), BF16),
            pltpu.VMEM((own_bands, panel), F32),
            pltpu.VMEM((panel, panel), F32),
            pltpu.VMEM((panel, panel), F32),
            pltpu.VMEM((panel, panel), BF16),
            pltpu.VMEM((panel, panel), BF16),
            pltpu.VMEM((panel, panel), BF16),
            pltpu.VMEM((panel, panel), BF16),
            pltpu.VMEM((chunks, LANES, panel), BF16),
            pltpu.VMEM((chunks, LANES, panel), BF16),
            dma((2,)),
            dma((chunks,)),
            dma((chunks,)),
            dma((chunks,)),
            dma((grid_count // 2,)),
            dma((grid_count,)),
            dma((grid_count // 2,)),
            dma((chunks,)),
            dma((chunks,)),
            dma((chunks,)),
            dma((chunks,)),
        ],
        compiler_params=pltpu.CompilerParams(
            collective_id=0, has_side_effects=True, vmem_limit_bytes=56 * 1024 * 1024
        ),
    )(point_index.reshape(1, panel), orbitals, factor_panels)


def solution(mesh):
    in_specs = (P("grid", None), P("pt"), P("pt", None))
    out_specs = P("grid", "pt")
    body = functools.partial(on_device, mesh.shape["grid"], mesh.shape["pt"])
    return jax.shard_map(
        body, mesh=mesh, in_specs=in_specs, out_specs=out_specs, check_vma=False
    )
```

```python
import functools
import jax
import jax.numpy as jnp
from jax import lax
from jax.experimental import pallas as pl
from jax.experimental.pallas import tpu as pltpu
from jax.sharding import PartitionSpec as P

MESH = pl.DeviceIdType.MESH
F32, BF16 = jnp.float32, jnp.bfloat16
LANES = 128
PIECE = 64


def split(value):
    high = value.astype(BF16)
    return high, (value - high.astype(F32)).astype(BF16)


def dot(a, b):
    return jnp.dot(a, b, preferred_element_type=F32)


def exact_dot(a, b):
    return jnp.dot(a, b, preferred_element_type=F32, precision=lax.Precision.HIGHEST)


def invert_lower(low, inv):
    size = low.shape[0]
    blocks = size // LANES
    row = lax.broadcasted_iota(jnp.int32, (LANES, LANES), 0)
    col = lax.broadcasted_iota(jnp.int32, (LANES, LANES), 1)
    tiles, parts = [], []
    for i in range(blocks):
        at = slice(i * LANES, (i + 1) * LANES)
        tile = low[at, at]
        tiles.append(tile)
        parts.append(jnp.where(row == col, 1.0 / jnp.where(row == col, tile, 1.0), 0.0))
    half = 1
    level = 0
    while half < LANES:
        rb, cb = row >> level, col >> level
        mask = ((rb >> 1) == (cb >> 1)) & (rb > cb)
        mids = [exact_dot(jnp.where(mask, tiles[i], 0.0), parts[i]) for i in range(blocks)]
        parts = [parts[i] - exact_dot(parts[i], mids[i]) for i in range(blocks)]
        half *= 2
        level += 1
    inv[...] = jnp.zeros_like(inv)
    for i in range(blocks):
        at = slice(i * LANES, (i + 1) * LANES)
        inv[at, at] = parts[i]
    width = LANES
    while width < size:
        for start in range(0, size, 2 * width):
            top = slice(start, start + width)
            bottom = slice(start + width, start + 2 * width)
            mid = exact_dot(low[bottom, top], inv[top, top])
            inv[bottom, top] = -exact_dot(inv[bottom, bottom], mid)
        width *= 2


def kernel(
    grid_count, pt_count, index_ref, orb, fac, out,
    orb_v, fac_v, rows, points, gathered, low, inv, a_high, a_low, b_high, b_low, firsts, seconds,
    load_sem, own_sem, row_send, row_recv, sibling_recv, late_send, help_send, help_recv,
    point_send, point_recv, pass_send,
    first_send, first_recv, second_send, second_recv,
):
    me = lax.axis_index("grid")
    rank = lax.axis_index("pt")
    own_bands, grid_rows = orb.shape
    half_bands = own_bands // 2
    chunks = rows.shape[0]
    panel = index_ref.shape[1]
    rows_here = chunks * LANES
    partner = me + 1 - 2 * lax.rem(me, 2)
    chip = me - lax.rem(me, 2)
    pairs = grid_count // 2
    far = grid_count - 2
    last = pt_count - 1
    mine = lax.rem(pt_count - rank, 2)

    def block(g):
        return pl.ds(pl.multiple_of(g * half_bands, half_bands), half_bands)

    def half_of(h):
        return pl.ds(pl.multiple_of(h * half_bands, half_bands), half_bands)

    def far_one(i):
        return lax.rem(chip + 2 + i, grid_count)

    load_orb = pltpu.make_async_copy(orb, orb_v, load_sem.at[0])
    load_fac = pltpu.make_async_copy(fac, fac_v, load_sem.at[1])
    load_orb.start()

    barrier = pltpu.get_barrier_semaphore()

    @pl.loop(1, grid_count)
    def _(k):
        other = lax.rem(me + k, grid_count)
        pl.semaphore_signal(barrier, inc=1, device_id=(other, rank), device_id_type=MESH)

    @pl.when(rank > 0)
    def _():
        pl.semaphore_signal(barrier, inc=1, device_id=(me, rank - 1), device_id_type=MESH)

    @pl.when(rank < last)
    def _():
        pl.semaphore_signal(barrier, inc=1, device_id=(me, rank + 1), device_id_type=MESH)

    at_end = (rank == 0) | (rank == last)

    @pl.when(at_end)
    def _():
        pl.semaphore_wait(barrier, grid_count)

    @pl.when(jnp.logical_not(at_end))
    def _():
        pl.semaphore_wait(barrier, grid_count + 1)

    def row_cols(g, c):
        return pl.ds(pl.multiple_of(g * rows_here + c * LANES, LANES), LANES)

    def row_copy(c, h, target, send_sem, recv_sem):
        return pltpu.make_async_remote_copy(
            src_ref=orb.at[half_of(h), row_cols(target, c)],
            dst_ref=rows.at[c, h, block(me), :],
            send_sem=send_sem.at[c],
            recv_sem=recv_sem.at[c],
            device_id=(target, rank),
            device_id_type=MESH,
        )

    def send_rows(c):
        @pl.loop(0, far)
        def _(i):
            row_copy(c, mine, far_one(i), row_send, row_recv).start()

        row_copy(c, 0, partner, row_send, sibling_recv).start()
        row_copy(c, 1, partner, row_send, sibling_recv).start()

    send_rows(0)
    for c in range(chunks):
        for h in range(2):
            pltpu.make_async_copy(
                orb.at[half_of(h), row_cols(me, c)], rows.at[c, h, block(me), :], own_sem.at[c]
            ).start()
    load_fac.start()
    load_orb.wait()

    depth = min(1024, grid_rows)
    gathered[...] = jnp.zeros_like(gathered)

    @pl.loop(0, grid_rows // depth)
    def _(s):
        ids = lax.broadcasted_iota(jnp.int32, (depth, panel), 0) + s * depth
        hot = jnp.where(ids == index_ref[...], 1.0, 0.0).astype(BF16)
        gathered[...] += dot(orb_v[:, pl.ds(pl.multiple_of(s * depth, depth), depth)], hot)

    points[0, block(me), :] = gathered[0:half_bands, :].astype(BF16)
    points[1, block(me), :] = gathered[half_bands:own_bands, :].astype(BF16)

    def point_copy(g, target, send_sem):
        return pltpu.make_async_remote_copy(
            src_ref=points.at[:, block(g), :],
            dst_ref=points.at[:, block(g), :],
            send_sem=send_sem,
            recv_sem=point_recv.at[g],
            device_id=(target, rank),
            device_id_type=MESH,
        )

    @pl.loop(1, pairs)
    def _(k):
        point_copy(me, lax.rem(me + 2 * k, grid_count), point_send.at[k]).start()

    point_copy(me, partner, pass_send.at[0]).start()
    for c in range(1, chunks):
        send_rows(c)

    @pl.when(rank == last)
    def _():
        for c in range(chunks):

            @pl.loop(0, far)
            def _(i):
                row_copy(c, 1 - mine, far_one(i), late_send, help_recv).start()

    def settle(c, count, sem):
        part = rows.at[c, 0, pl.ds(0, count), :]
        pltpu.make_async_copy(part, part, sem.at[c]).wait()

    def forward(c):
        settle(c, far * half_bands, row_recv)

        @pl.when(rank > 0)
        def _():
            @pl.loop(0, far)
            def _(i):
                part = rows.at[c, mine, block(far_one(i)), :]
                pltpu.make_async_remote_copy(
                    src_ref=part,
                    dst_ref=part,
                    send_sem=help_send.at[c],
                    recv_sem=help_recv.at[c],
                    device_id=(me, rank - 1),
                    device_id_type=MESH,
                ).start()

    @pl.when(rank > 0)
    def _():
        forward(0)

    load_fac.wait()

    @pl.when(rank < 2)
    def _():
        start = pl.multiple_of(rank * panel, panel)
        low[...] = fac_v[:, pl.ds(start, panel)]
        invert_lower(low, inv)

    @pl.when(rank > 0)
    def _():
        a_high[...], a_low[...] = split(fac_v[:, 0:panel].T)

    @pl.when(rank == 0)
    def _():
        a_high[...], a_low[...] = split(inv[...].T)

    @pl.when(rank > 1)
    def _():
        b_high[...], b_low[...] = split(fac_v[:, panel : 2 * panel].T)

    @pl.when(rank == 1)
    def _():
        b_high[...], b_low[...] = split(inv[...].T)

    @pl.loop(1, pairs)
    def _(k):
        source = lax.rem(me + 2 * (pairs - k), grid_count)
        point_copy(source, me, point_send.at[k]).wait_recv()
        point_copy(source, partner, pass_send.at[k]).start()

    for c in range(1, chunks):

        @pl.when(rank > c)
        def _():
            forward(c)

    @pl.loop(0, pairs)
    def _(k):
        source = lax.rem(partner + 2 * k, grid_count)
        point_copy(source, me, pass_send.at[k]).wait_recv()

    def chain(buf, p, send_sem, recv_sem):
        return pltpu.make_async_remote_copy(
            src_ref=buf.at[p],
            dst_ref=buf.at[p],
            send_sem=send_sem.at[p],
            recv_sem=recv_sem.at[p],
            device_id=(me, rank + 1),
            device_id_type=MESH,
        )

    def solve(value, high, low_part):
        value_high, value_low = split(value)
        return dot(value_high, high[...]) + (dot(value_high, low_part[...]) + dot(value_low, high[...]))

    def apply(value, high, low_part):
        return dot(value, high[...]) + dot(value, low_part[...])

    piece = firsts.shape[1]
    pieces = LANES // piece

    @pl.loop(0, chunks)
    def _(c):
        @pl.when(c + rank < chunks)
        def _():
            forward(c + rank)

        settle(c, own_bands, own_sem)
        settle(c, own_bands, sibling_recv)
        settle(c, far * half_bands, help_recv)
        over_bands = (((0,), (0,)), ((), ()))
        sums = lax.dot_general(rows[c, 0], points[0], over_bands, preferred_element_type=F32)
        sums += lax.dot_general(rows[c, 1], points[1], over_bands, preferred_element_type=F32)
        out[pl.ds(pl.multiple_of(c * LANES, LANES), LANES), :] = sums * sums

        @pl.loop(c * pieces, (c + 1) * pieces)
        def _(p):
            here = pl.ds(pl.multiple_of(p * piece, piece), piece)

            @pl.when(rank == 0)
            def _():
                first = solve(out[here, :], a_high, a_low)
                out[here, :] = first
                firsts[p] = first.astype(BF16)

            @pl.when(rank > 0)
            def _():
                chain(firsts, p, first_send, first_recv).wait_recv()

            @pl.when(rank < last)
            def _():
                chain(firsts, p, first_send, first_recv).start()

            @pl.when(rank > 0)
            def _():
                out[here, :] -= apply(firsts[p], a_high, a_low)

            @pl.when(rank == 1)
            def _():
                second = solve(out[here, :], b_high, b_low)
                out[here, :] = second
                seconds[p] = second.astype(BF16)

            @pl.when(rank > 1)
            def _():
                chain(seconds, p, second_send, second_recv).wait_recv()

            @pl.when((rank > 0) & (rank < last))
            def _():
                chain(seconds, p, second_send, second_recv).start()

            @pl.when(rank > 1)
            def _():
                out[here, :] -= apply(seconds[p], b_high, b_low)

    @pl.loop(0, chunks)
    def _(c):
        settle(c, grid_count * half_bands, row_send)

        @pl.when(rank == last)
        def _():
            settle(c, far * half_bands, late_send)

        @pl.when(rank > 0)
        def _():
            settle(c, far * half_bands, help_send)

    @pl.loop(0, chunks * pieces)
    def _(p):
        @pl.when(rank < last)
        def _():
            chain(firsts, p, first_send, first_recv).wait_send()

        @pl.when((rank > 0) & (rank < last))
        def _():
            chain(seconds, p, second_send, second_recv).wait_send()

    @pl.loop(1, pairs)
    def _(k):
        point_copy(me, partner, point_send.at[k]).wait_send()

    @pl.loop(0, pairs)
    def _(k):
        point_copy(me, partner, pass_send.at[k]).wait_send()


def on_device(grid_count, pt_count, orbitals, point_index, factor_panels):
    own_bands, grid_rows = orbitals.shape
    rows_here = grid_rows // grid_count
    panel = point_index.shape[0]
    chunks = rows_here // LANES
    bands = own_bands * grid_count
    vmem = pl.BlockSpec(memory_space=pltpu.VMEM)
    hbm = pl.BlockSpec(memory_space=pl.ANY)
    dma = pltpu.SemaphoreType.DMA
    return pl.pallas_call(
        functools.partial(kernel, grid_count, pt_count),
        out_shape=jax.ShapeDtypeStruct((rows_here, panel), F32),
        in_specs=[vmem, hbm, hbm],
        out_specs=vmem,
        scratch_shapes=[
            pltpu.VMEM((own_bands, grid_rows), BF16),
            pltpu.VMEM(factor_panels.shape, F32),
            pltpu.VMEM((chunks, 2, bands // 2, LANES), BF16),
            pltpu.VMEM((2, bands // 2, panel), BF16),
            pltpu.VMEM((own_bands, panel), F32),
            pltpu.VMEM((panel, panel), F32),
            pltpu.VMEM((panel, panel), F32),
            pltpu.VMEM((panel, panel), BF16),
            pltpu.VMEM((panel, panel), BF16),
            pltpu.VMEM((panel, panel), BF16),
            pltpu.VMEM((panel, panel), BF16),
            pltpu.VMEM((rows_here // PIECE, PIECE, panel), BF16),
            pltpu.VMEM((rows_here // PIECE, PIECE, panel), BF16),
            dma((2,)),
            *[dma((chunks,))] * 7,
            dma((grid_count // 2,)),
            dma((grid_count,)),
            dma((grid_count // 2,)),
            *[dma((rows_here // PIECE,))] * 4,
        ],
        compiler_params=pltpu.CompilerParams(
            collective_id=0, has_side_effects=True, vmem_limit_bytes=56 * 1024 * 1024
        ),
    )(point_index.reshape(1, panel), orbitals, factor_panels)


def solution(mesh):
    in_specs = (P("grid", None), P("pt"), P("pt", None))
    out_specs = P("grid", "pt")
    body = functools.partial(on_device, mesh.shape["grid"], mesh.shape["pt"])
    return jax.shard_map(
        body, mesh=mesh, in_specs=in_specs, out_specs=out_specs, check_vma=False
    )
```
